32 devices in a mesh: dp: 4 (over x, core), expert: 8 (over z, y).
Axes of the slice: x: 2, y: 2, z: 4, core: 2. Of those that a mesh axis runs over, the one named last changes fastest.
Arguments:
- dense_weights: bfloat16 [3, 5632, 2048], P(None, 'dp', 'expert'), may hold values from -0.125 to 0.125
- tokens: bfloat16 [1024, 2048], P('expert'), may hold values from -6 to 6
- cotangent: bfloat16 [1024, 2048], P('expert'), may hold values from -6 to 6
- routes: int32 [1024, 4], P('expert'), may hold values from 0 to 7, all different within a row; in each aligned block of 128 rows (0 to 127, 128 to 255, ...) at most 80 rows name the same one
- route_gates: float32 [1024, 4], P('expert'), may hold values from 0.2 to 1
- unit_perm: int32 [2, 5632], replicated, may hold values from 0 to 5631, as said below
- slab_owner: int32 [8], replicated, may hold values from 0 to 7, each once
Outputs:
- mixed: bfloat16 [1024, 2048], P('expert', 'dp')
- token_grad: bfloat16 [1024, 2048], P('expert', 'dp')
- expert_grad: bfloat16 [8, 3, 1408, 2048], P('expert', None, 'dp')
The draws below stay inside these ranges and needn't reach their ends.
Inputs may be any that keep to these rules, and one draw needn't show every extreme that they name: `unit_perm`: each row is a permutation of the 5632 units. In every row, for every slab s and share g, the 352 positions s * 1408 + g * 352 up to s * 1408 + (g + 1) * 352 - 1 hold exactly 88 units of each block of 1408 consecutive units. `slab_owner`: each slab number c * 4 + s is owned by exactly one expert. `routes`: each row names 4 different experts. In each aligned block of 128 rows no expert is named more than 80 times, a bound that some block reaches.
All inputs are finite; a program needn't handle non-finite values.
Results may differ from the reference program's by a relative error of at most 0.013.
Values may be sent and summed in bfloat16 or wider, within the bound.
A program may use at most 128 MiB of HBM per device.

```python
import math
import jax
import jax.numpy as jnp
import numpy as np
from jax import lax

D = 2048
FF = 5632
EH = 1408
TOPK = 4
TOK_DEV = 128
EXPERTS = 8
SLABS = 4
COPIES = 2
UNITS_DEV = 352
PICK = 88
CAP = 80
TOKENS = 1024
N_DP = 4
N_EXPERT = 8


def draw_unit_perm(key, part):
    block_units = FF // N_DP
    key_list = jax.random.split(key, COPIES * N_DP)
    local_order = jax.vmap(lambda subkey: jax.random.permutation(subkey, block_units))(key_list)
    local_order = local_order.reshape(COPIES, N_DP, SLABS * N_DP, PICK).astype(jnp.int32)
    offsets = (jnp.arange(N_DP, dtype=jnp.int32) * block_units)[None, :, None, None]
    unit_ids = local_order + offsets
    unit_ids = jnp.transpose(unit_ids, (0, 2, 1, 3)).reshape(COPIES, SLABS * N_DP, UNITS_DEV)
    second_keys = jax.random.split(jax.random.fold_in(key, 7), COPIES * SLABS * N_DP)
    pair_order = jax.vmap(lambda subkey: jax.random.permutation(subkey, UNITS_DEV))(second_keys)
    pair_order = pair_order.reshape(COPIES, SLABS * N_DP, UNITS_DEV).astype(jnp.int32)
    unit_ids = jnp.take_along_axis(unit_ids, pair_order, axis=2)
    return unit_ids.reshape(COPIES, FF).astype(jnp.int32)


def block_scale(stream_key, shape, cuts, least, largest):
    def one(axis_at, parts):
        draws = jax.random.uniform(jax.random.fold_in(jax.random.fold_in(stream_key, 6), axis_at), (parts,), jnp.float32, least / len(cuts), largest / len(cuts))
        return jnp.repeat(jnp.exp(draws), shape[axis_at] // parts).reshape((-1,) + (1,) * (len(shape) - axis_at - 1))

    level = one(*cuts[0])
    for cut in cuts[1:]:
        level = level * one(*cut)
    return level


def assign_block(rng, own, number, rows, amount, top, bound, slope):
    order = jax.random.permutation(rng, amount)
    crowded, usual = shares(amount, rows * top, bound, slope, True), shares(amount, rows * top, bound, slope, False)
    places = jnp.arange(amount)

    def named(lengths, offset_by):
        used = int((lengths > 0).sum())
        fixed = max(1, used // 4)
        shifted = fixed + (places - fixed + offset_by * (used - fixed)) % max(1, amount - fixed)
        return jnp.zeros((amount,), jnp.int32).at[order[jnp.where(places < fixed, places, shifted)]].set(jnp.asarray(lengths, jnp.int32))

    lengths = jnp.where(number % 4 == 0, named(crowded, number // 4), named(usual, number - number // 4 - 1))
    mixed = jax.random.permutation(jax.random.fold_in(own, 3), amount)
    giver, sink = mixed[0:amount // 2 * 2:2], mixed[1:amount // 2 * 2:2]
    slack = jnp.minimum(lengths[giver] - 1, bound - lengths[sink]) // 2
    slack = jnp.where((giver == order[0]) | (sink == order[0]) | (lengths[sink] == 0), 0, jnp.maximum(slack, 0))
    shifted = jax.random.randint(jax.random.fold_in(own, 4), (amount // 2,), 0, 1 << 20) % (slack + 1)
    lengths = lengths.at[giver].add(-shifted).at[sink].add(shifted)
    labels = jnp.searchsorted(jnp.cumsum(lengths), jnp.arange(rows * top), side="right").astype(jnp.int32)
    table = labels.reshape(top, rows).T
    table = table[jax.random.permutation(jax.random.fold_in(own, 1), rows)]
    offset_by = jax.random.randint(jax.random.fold_in(own, 2), (rows, 1), 0, top)
    return jnp.take_along_axis(table, (jnp.arange(top)[None, :] + offset_by) % top, axis=1)


def shares(number_of, total, bound, slope, full):
    loads = [(1 << 20) // math.isqrt(grade ** slope) + 1 for grade in range(1, number_of + 1)]
    largest = bound if full else min(bound, max(-(-total // number_of), total * loads[0] // sum(loads)))
    least = 1 if total - largest >= number_of - 1 else 0
    given, spare = [largest] + [least] * (number_of - 1), total - largest - least * (number_of - 1)
    while spare > 0:
        movable = [i for i in range(1, number_of) if given[i] < largest] or [i for i in range(1, number_of) if given[i] < bound]
        pool, left = sum([loads[i] for i in movable]), spare
        for i in movable:
            addition = min(bound - given[i], max(1, left * loads[i] // pool), spare)
            given[i] = given[i] + addition
            spare = spare - addition
    return np.array(given)


def gaussian(rng, extent, scale, most, pieces=(), kind=jnp.bfloat16):
    loudness = block_scale(rng, extent, pieces, -0.22, 0.18) if pieces else 1.0
    values = jax.random.normal(rng, extent, jnp.float32) * scale * loudness
    return jnp.minimum(jnp.maximum(values, -most), most).astype(kind)


def setup_inputs(seed: int = 0) -> dict:
    streams_of = jax.random.split(jax.random.key(seed), 8)
    dense_weights = gaussian(streams_of[0], (3, FF, D), D ** -0.5, 0.125, ((1, 4), (2, 8)))
    tokens = gaussian(streams_of[1], (TOKENS, D), 1.0, 6.0, ((0, 8),))
    cotangent = gaussian(streams_of[2], (TOKENS, D), 1.0, 6.0, ((0, 8),))
    routes_keys = jax.random.split(jax.random.fold_in(streams_of[3], 1), TOKENS // TOK_DEV)
    routes_turns = jax.random.permutation(jax.random.fold_in(streams_of[3], 3), TOKENS // TOK_DEV)
    routes = jax.vmap(lambda own, number: assign_block(jax.random.fold_in(streams_of[3], 2), own, number, TOK_DEV, EXPERTS, TOPK, CAP, 1))(routes_keys, routes_turns).reshape((TOKENS, TOPK))
    route_gates = jnp.clip(0.2 + 0.8 * jax.random.uniform(streams_of[4], (TOKENS, TOPK), jnp.float32) ** block_scale(streams_of[4], (TOKENS, TOPK), ((0, 8),), -0.2, 0.2), 0.2, 1.0)
    unit_perm = draw_unit_perm(jax.random.fold_in(streams_of[7], 71), 0)
    slab_owner = jax.random.permutation(streams_of[6], EXPERTS).astype(jnp.int32)
    return dict(dense_weights=dense_weights, tokens=tokens, cotangent=cotangent, routes=routes, route_gates=route_gates, unit_perm=unit_perm, slab_owner=slab_owner)


def silu_parts(preact):
    sigmoid_value = jax.nn.sigmoid(preact)
    return preact * sigmoid_value, sigmoid_value * (1.0 + preact * (1.0 - sigmoid_value))


def share_products(left_side, weights):
    left_f = left_side.astype(jnp.float32).reshape(left_side.shape[0], N_DP, UNITS_DEV)
    right_f = weights.astype(jnp.float32).reshape(N_DP, UNITS_DEV, D)
    return jnp.einsum("sgu,gud->sgd", left_f, right_f)


def round_sum(share_parts):
    rounded = lax.optimization_barrier(share_parts.astype(jnp.bfloat16))
    return jnp.sum(rounded.astype(jnp.float32), axis=1)


def reference(dense_weights, tokens, cotangent, routes, route_gates, unit_perm, slab_owner):
    shared_gate = jnp.dot(tokens, dense_weights[0].T, preferred_element_type=jnp.float32)
    shared_up = jnp.dot(tokens, dense_weights[1].T, preferred_element_type=jnp.float32)
    shared_act, shared_slope = silu_parts(shared_gate)
    shared_hidden = (shared_act * shared_up).astype(jnp.bfloat16)
    shared_out = jnp.dot(shared_hidden, dense_weights[2], preferred_element_type=jnp.float32)
    shared_dh = jnp.dot(cotangent, dense_weights[2].T, preferred_element_type=jnp.float32)
    shared_dgate = (shared_dh * shared_up * shared_slope).astype(jnp.bfloat16)
    shared_dup = (shared_dh * shared_act).astype(jnp.bfloat16)
    shared_back = jnp.dot(shared_dgate, dense_weights[0], preferred_element_type=jnp.float32) + jnp.dot(shared_dup, dense_weights[1], preferred_element_type=jnp.float32)

    copies = TOKENS * TOPK
    flat_routes = routes.reshape(-1).astype(jnp.int32)
    onehot = (flat_routes[:, None] == jnp.arange(EXPERTS, dtype=jnp.int32)[None, :]).astype(jnp.int32)
    running = jnp.cumsum(onehot.reshape(N_EXPERT, TOK_DEV * TOPK, EXPERTS), axis=1).reshape(copies, EXPERTS)
    slot_rank = jnp.sum((running - 1) * onehot, axis=1)
    block_of = jnp.arange(copies, dtype=jnp.int32) // (TOK_DEV * TOPK)
    slot_index = (block_of * CAP + slot_rank).astype(jnp.int32)
    slot_table = jnp.full((EXPERTS, N_EXPERT * CAP), copies, jnp.int32).at[flat_routes, slot_index].set(jnp.arange(copies, dtype=jnp.int32))
    flat_gates = route_gates.reshape(-1)

    def expert_step(packed):
        expert, slot_rows = packed
        owned_slab = slab_owner[expert]
        copy_id = (owned_slab // SLABS).astype(jnp.int32)
        slab_start = ((owned_slab % SLABS) * EH).astype(jnp.int32)
        unit_ids = lax.dynamic_slice(unit_perm, (copy_id, slab_start), (1, EH))[0]
        weights = jnp.take(dense_weights, unit_ids, axis=1)
        filled = slot_rows < copies
        safe_rows = jnp.minimum(slot_rows, copies - 1)
        token_of = safe_rows // TOPK
        copy_x = jnp.where(filled[:, None], tokens[token_of], jnp.zeros((), jnp.bfloat16))
        gate_of = jnp.where(filled, flat_gates[safe_rows], jnp.zeros((), jnp.float32))
        copy_dy = (gate_of[:, None] * cotangent[token_of].astype(jnp.float32)).astype(jnp.bfloat16)
        pre_gate = jnp.dot(copy_x, weights[0].T, preferred_element_type=jnp.float32)
        pre_up = jnp.dot(copy_x, weights[1].T, preferred_element_type=jnp.float32)
        activation, silu_slope = silu_parts(pre_gate)
        hidden = (activation * pre_up).astype(jnp.bfloat16)
        out_rows = round_sum(share_products(hidden, weights[2]))
        d_hidden = jnp.dot(copy_dy, weights[2].T, preferred_element_type=jnp.float32)
        d_gate = (d_hidden * pre_up * silu_slope).astype(jnp.bfloat16)
        d_up = (d_hidden * activation).astype(jnp.bfloat16)
        back_rows = round_sum(share_products(d_gate, weights[0]) + share_products(d_up, weights[1]))
        weight_grads = jnp.stack([
            jnp.dot(d_gate.T, copy_x, preferred_element_type=jnp.float32),
            jnp.dot(d_up.T, copy_x, preferred_element_type=jnp.float32),
            jnp.dot(hidden.T, copy_dy, preferred_element_type=jnp.float32),
        ]).astype(jnp.bfloat16)
        return out_rows, back_rows, weight_grads

    out_rows, back_rows, expert_grad = lax.map(expert_step, (jnp.arange(EXPERTS, dtype=jnp.int32), slot_table))
    routed_out = out_rows[flat_routes, slot_index].reshape(TOKENS, TOPK, D)
    routed_back = back_rows[flat_routes, slot_index].reshape(TOKENS, TOPK, D)
    mixed = (shared_out + jnp.sum(route_gates[:, :, None] * routed_out, axis=1)).astype(jnp.bfloat16)
    token_grad = (shared_back + jnp.sum(routed_back, axis=1)).astype(jnp.bfloat16)
    return mixed, token_grad, expert_grad
```

```python
import jax
import jax.numpy as jnp
from jax import lax
from jax.sharding import PartitionSpec as P

F32 = jnp.float32
BF16 = jnp.bfloat16


def silu_parts(preact):
    sigmoid_value = jax.nn.sigmoid(preact)
    return (preact * sigmoid_value, sigmoid_value * (1.0 + preact * (1.0 - sigmoid_value)))


def dot(left, right, left_dim, right_dim):
    return lax.dot_general(
        left, right, (((left_dim,), (right_dim,)), ((), ())), preferred_element_type=F32
    )


def block_ranks(blocks, block):
    width = blocks.shape[-1]
    mask = blocks == block
    upper = lax.broadcasted_iota(jnp.int32, (width, width), 0) < lax.broadcasted_iota(
        jnp.int32, (width, width), 1
    )
    rank = jnp.dot(mask.astype(BF16), upper.astype(BF16), preferred_element_type=F32)
    return mask, rank.astype(jnp.int32)


def body(dense_weights, tokens, cotangent, routes, route_gates, unit_perm, slab_owner):
    n_dp = lax.axis_size("dp")
    n_ex = lax.axis_size("expert")
    row = lax.axis_index("dp")
    col = lax.axis_index("expert")
    _, block_units, feat = dense_weights.shape
    copies, total_units = unit_perm.shape
    slabs = n_ex // copies
    slab_units = total_units // slabs
    share = slab_units // n_dp
    pick = share // n_dp
    tok, width = tokens.shape

    shares = unit_perm.reshape(n_ex, n_dp, share)
    dest = jnp.transpose(shares[slab_owner], (1, 0, 2)).reshape(n_dp * n_ex, share)
    mask, rank = block_ranks(dest // block_units, row)
    place = jnp.where(mask, rank, -1)
    hit = place[:, None, :] == lax.broadcasted_iota(jnp.int32, (1, pick, 1), 1)
    units = jnp.sum(jnp.where(hit, (dest - row * block_units)[:, None, :], 0), axis=2)
    onehot = (
        units.reshape(-1, 1) == lax.broadcasted_iota(jnp.int32, (1, block_units), 1)
    ).astype(BF16)
    picked = dot(onehot, dense_weights, 1, 1).astype(BF16)
    picked = picked.reshape(n_dp * n_ex, pick, 3 * feat)
    arrived = lax.all_to_all(picked, ("dp", "expert"), split_axis=0, concat_axis=0, tiled=True)
    arrived = arrived.reshape(n_dp, n_ex, pick, 3, feat)
    weights = jnp.transpose(arrived, (3, 0, 2, 1, 4)).reshape(3, share, width)
    w_gate, w_up, w_down = weights[0], weights[1], weights[2]

    mine = lax.dynamic_slice(
        shares, (slab_owner[col], row, 0), (1, 1, share)
    ).reshape(1, share)
    mine_block = mine // block_units
    mask, rank = block_ranks(
        jnp.broadcast_to(mine_block, (n_dp, share)),
        lax.broadcasted_iota(jnp.int32, (n_dp, 1), 0),
    )
    at = jnp.sum(
        jnp.where(mask, rank + lax.broadcasted_iota(jnp.int32, (n_dp, 1), 0) * pick, 0), axis=0
    )
    order = (lax.broadcasted_iota(jnp.int32, (share, share), 0) == at[None, :]).astype(BF16)

    part = width // n_dp
    both = jnp.concatenate(
        [
            lax.dynamic_slice(tokens, (0, row * part), (tok, part)),
            lax.dynamic_slice(cotangent, (0, row * part), (tok, part)),
        ],
        axis=1,
    )
    both = lax.all_gather(both, "expert", axis=0, tiled=True)
    both = lax.all_gather(both, "dp", axis=0, tiled=False)
    all_x = jnp.transpose(both[:, :, :part], (1, 0, 2)).reshape(n_ex * tok, width)
    all_c = jnp.transpose(both[:, :, part:], (1, 0, 2)).reshape(n_ex * tok, width)

    gate_table = jnp.sum(
        jnp.where(
            routes[None, :, :] == lax.broadcasted_iota(jnp.int32, (n_ex, 1, 1), 0),
            route_gates[None, :, :],
            0.0,
        ),
        axis=2,
    )
    gate = lax.all_to_all(gate_table, "expert", split_axis=0, concat_axis=0, tiled=True)
    gate = gate.reshape(n_ex * tok, 1)
    copy_id = slab_owner[col] // slabs
    owner_block = lax.broadcasted_iota(jnp.int32, (n_ex, tok), 0).reshape(n_ex * tok, 1)
    both_weight = gate + (owner_block * copies // n_ex == copy_id).astype(F32)

    pre_gate = dot(all_x, w_gate, 1, 1)
    pre_up = dot(all_x, w_up, 1, 1)
    d_hidden = dot(all_c, w_down, 1, 1)
    act, slope = silu_parts(pre_gate)
    hidden = act * pre_up
    d_gate = d_hidden * pre_up * slope
    d_up = d_hidden * act

    out = dot((both_weight * hidden).astype(BF16), w_down, 1, 0).astype(BF16)
    back = (
        dot((both_weight * d_gate).astype(BF16), w_gate, 1, 0)
        + dot((both_weight * d_up).astype(BF16), w_up, 1, 0)
    ).astype(BF16)

    def grad(values, rows):
        ordered = jnp.dot((gate * values).astype(BF16), order, preferred_element_type=F32)
        return dot(ordered.astype(BF16), rows, 0, 0)

    weight_grads = jnp.stack(
        [grad(d_gate, all_x), grad(d_up, all_x), grad(hidden, all_c)]
    ).astype(BF16)[None]

    def collect(partial):
        partial = lax.psum_scatter(partial, "dp", scatter_dimension=1, tiled=True)
        return lax.psum_scatter(partial, "expert", scatter_dimension=0, tiled=True)

    return (collect(out), collect(back), weight_grads)


def solution(mesh):
    in_specs = (
        P(None, "dp", "expert"),
        P("expert", None),
        P("expert", None),
        P("expert", None),
        P("expert", None),
        P(),
        P(),
    )
    out_specs = (P("expert", "dp"), P("expert", "dp"), P("expert", None, "dp", None))
    return jax.shard_map(body, mesh=mesh, in_specs=in_specs, out_specs=out_specs, check_vma=False)
```

```python
import functools

import jax
import jax.numpy as jnp
from jax import lax
from jax.experimental import pallas as pl
from jax.experimental.pallas import tpu as pltpu
from jax.sharding import PartitionSpec as P

F32 = jnp.float32
BF16 = jnp.bfloat16


def silu_parts(preact):
    sigmoid_value = jax.nn.sigmoid(preact)
    return (preact * sigmoid_value, sigmoid_value * (1.0 + preact * (1.0 - sigmoid_value)))


def dot(left, right, left_dim, right_dim):
    return lax.dot_general(
        left, right, (((left_dim,), (right_dim,)), ((), ())), preferred_element_type=F32
    )


def block_ranks(blocks, block):
    width = blocks.shape[-1]
    mask = blocks == block
    upper = lax.broadcasted_iota(jnp.int32, (width, width), 0) < lax.broadcasted_iota(
        jnp.int32, (width, width), 1
    )
    rank = jnp.dot(mask.astype(BF16), upper.astype(BF16), preferred_element_type=F32)
    return mask, rank.astype(jnp.int32)


def log2(count):
    return count.bit_length() - 1


def flip(index, place):
    return index + (1 - 2 * (index // (1 << place) % 2)) * (1 << place)


def peer(device, n_ex):
    return {"dp": device // n_ex, "expert": device % n_ex}


STREAMS = 4


def halving_orders(dp_bits, ex_bits):
    rest = [ex_bits + bit for bit in range(1, dp_bits)] + list(range(ex_bits))
    turns = [[0, 1, 2], [1, 2, 0], [2, 0, 1], [1, 0, 2]]
    orders = []
    for turn in turns:
        head = [rest[at] for at in turn if at < len(rest)]
        orders.append([ex_bits] + head + rest[len(head) :])
    return orders


def halving_kernel(n_dp, n_ex, n_arrays, *refs):
    ins, outs = refs[:n_arrays], refs[n_arrays : 2 * n_arrays]
    data, recv, load_sem, send_sem, recv_sem = refs[2 * n_arrays :]
    me = lax.axis_index("dp") * n_ex + lax.axis_index("expert")
    bits = log2(n_dp) + log2(n_ex)
    orders = halving_orders(log2(n_dp), log2(n_ex))
    rows, part = data.shape[2:]
    splits = STREAMS // n_arrays

    for stream in range(STREAMS):
        source, at = ins[stream // splits], stream % splits
        for g in range(n_dp):

            def load(e, carry, source=source, at=at, g=g, stream=stream):
                start = pl.multiple_of(e * (rows * splits) + at * rows, rows)
                pltpu.make_async_copy(
                    source.at[pl.ds(start, rows), pl.ds(g * part, part)],
                    data.at[stream, g * n_ex + e],
                    load_sem.at[stream],
                ).start()
                return carry

            lax.fori_loop(0, n_ex, load, 0)

    barrier = pltpu.get_barrier_semaphore()
    for place in range(bits):
        pl.semaphore_signal(
            barrier,
            inc=1,
            device_id=peer(flip(me, place), n_ex),
            device_id_type=pl.DeviceIdType.MESH,
        )
    pl.semaphore_wait(barrier, bits)

    def block_of(stream, step, choice, sent):
        order = orders[stream]
        index = 0
        for place in order[: step + 1]:
            index = index + me // (1 << place) % 2 * (1 << place)
        if sent:
            index = flip(index, order[step])
        for bit, place in enumerate(sorted(order[step + 1 :])):
            index = index + choice // (1 << bit) % 2 * (1 << place)
        return index

    def count(step):
        return 1 << (bits - 1 - step)

    def offset(step):
        return (1 << bits) - (1 << (bits - step))

    def send(stream, step, choice):
        pltpu.make_async_remote_copy(
            src_ref=data.at[stream, block_of(stream, step, choice, True)],
            dst_ref=recv.at[stream, offset(step) + choice],
            send_sem=send_sem.at[stream, step],
            recv_sem=recv_sem.at[stream, step],
            device_id=peer(flip(me, orders[stream][step]), n_ex),
            device_id_type=pl.DeviceIdType.MESH,
        ).start()

    def region(stream, step):
        view = recv.at[stream, pl.ds(offset(step), count(step))]
        return pltpu.make_async_remote_copy(
            src_ref=view,
            dst_ref=view,
            send_sem=send_sem.at[stream, step],
            recv_sem=recv_sem.at[stream, step],
            device_id=peer(flip(me, orders[stream][step]), n_ex),
            device_id_type=pl.DeviceIdType.MESH,
        )

    def number(stream, step, choice, sent):
        order = orders[stream]
        later = sorted(order[step + 1 :])
        place = order[step + 1]
        mine = me // (1 << place) % 2
        value = (1 - mine if sent else mine) * (1 << later.index(place))
        for bit, other in enumerate(sorted(order[step + 2 :])):
            value = value + choice // (1 << bit) % 2 * (1 << later.index(other))
        return value

    for stream in range(STREAMS):
        pltpu.make_async_copy(data.at[stream], data.at[stream], load_sem.at[stream]).wait()

        def first(choice, carry, stream=stream):
            send(stream, 0, choice)
            return carry

        lax.fori_loop(0, count(0), first, 0)

    for step in range(bits):
        for stream in range(STREAMS):
            region(stream, step).wait_recv()
            if step == bits - 1:
                total = data[stream, me].astype(F32) + recv[stream, offset(step)].astype(F32)
                outs[stream // splits][pl.ds(stream % splits * rows, rows), :] = total.astype(BF16)
                continue
            for sent in (True, False):

                def add(choice, carry, stream=stream, step=step, sent=sent):
                    block = block_of(stream, step + 1, choice, sent)
                    slot = offset(step) + number(stream, step, choice, sent)
                    total = data[stream, block].astype(F32) + recv[stream, slot].astype(F32)
                    data[stream, block] = total.astype(BF16)
                    if sent:
                        send(stream, step + 1, choice)
                    return carry

                lax.fori_loop(0, count(step + 1), add, 0)

    for step in range(bits):
        for stream in range(STREAMS):
            region(stream, step).wait_send()


def halving_sum(n_dp, n_ex, arrays):
    total, width = arrays[0].shape
    tok, part, n_arrays = total // n_ex, width // n_dp, len(arrays)
    rows = tok * n_arrays // STREAMS
    blocks = n_dp * n_ex
    steps = log2(blocks)
    return pl.pallas_call(
        functools.partial(halving_kernel, n_dp, n_ex, n_arrays),
        out_shape=[jax.ShapeDtypeStruct((tok, part), BF16)] * n_arrays,
        in_specs=[pl.BlockSpec(memory_space=pl.ANY)] * n_arrays,
        out_specs=[pl.BlockSpec(memory_space=pltpu.VMEM)] * n_arrays,
        scratch_shapes=[
            pltpu.VMEM((STREAMS, blocks, rows, part), BF16),
            pltpu.VMEM((STREAMS, blocks - 1, rows, part), BF16),
            pltpu.SemaphoreType.DMA((STREAMS,)),
            pltpu.SemaphoreType.DMA((STREAMS, steps)),
            pltpu.SemaphoreType.DMA((STREAMS, steps)),
        ],
        compiler_params=pltpu.CompilerParams(
            collective_id=1, has_side_effects=True, vmem_limit_bytes=60 << 20
        ),
        name="halving_sum",
    )(*arrays)


def body(dense_weights, tokens, cotangent, routes, route_gates, unit_perm, slab_owner):
    n_dp = lax.axis_size("dp")
    n_ex = lax.axis_size("expert")
    row = lax.axis_index("dp")
    col = lax.axis_index("expert")
    _, block_units, feat = dense_weights.shape
    copies, total_units = unit_perm.shape
    slabs = n_ex // copies
    slab_units = total_units // slabs
    share = slab_units // n_dp
    pick = share // n_dp
    tok, width = tokens.shape

    shares = unit_perm.reshape(n_ex, n_dp, share)
    dest = jnp.transpose(shares[slab_owner], (1, 0, 2)).reshape(n_dp * n_ex, share)
    mask, rank = block_ranks(dest // block_units, row)
    place = jnp.where(mask, rank, -1)
    hit = place[:, None, :] == lax.broadcasted_iota(jnp.int32, (1, pick, 1), 1)
    units = jnp.sum(jnp.where(hit, (dest - row * block_units)[:, None, :], 0), axis=2)
    onehot = (
        units.reshape(-1, 1) == lax.broadcasted_iota(jnp.int32, (1, block_units), 1)
    ).astype(BF16)
    side = jnp.concatenate([dense_weights[0], dense_weights[1], dense_weights[2]], axis=1)
    picked = dot(onehot, side, 1, 0).astype(BF16)
    picked = picked.reshape(n_dp * n_ex, pick, 3 * feat)
    arrived = lax.all_to_all(picked, ("dp", "expert"), split_axis=0, concat_axis=0, tiled=True)
    arrived = arrived.reshape(n_dp, n_ex, pick, 3, feat)
    weights = jnp.transpose(arrived, (3, 0, 2, 1, 4)).reshape(3, share, width)
    w_gate, w_up, w_down = weights[0], weights[1], weights[2]

    mine = lax.dynamic_slice(
        shares, (slab_owner[col], row, 0), (1, 1, share)
    ).reshape(1, share)
    mine_block = mine // block_units
    mask, rank = block_ranks(
        jnp.broadcast_to(mine_block, (n_dp, share)),
        lax.broadcasted_iota(jnp.int32, (n_dp, 1), 0),
    )
    at = jnp.sum(
        jnp.where(mask, rank + lax.broadcasted_iota(jnp.int32, (n_dp, 1), 0) * pick, 0), axis=0
    )
    order = (lax.broadcasted_iota(jnp.int32, (share, share), 0) == at[None, :]).astype(BF16)

    part = width // n_dp
    both = jnp.concatenate(
        [
            lax.dynamic_slice(tokens, (0, row * part), (tok, part)),
            lax.dynamic_slice(cotangent, (0, row * part), (tok, part)),
        ],
        axis=1,
    )
    both = lax.all_gather(both, "expert", axis=0, tiled=True)
    both = lax.all_gather(both, "dp", axis=0, tiled=False)
    all_x = jnp.transpose(both[:, :, :part], (1, 0, 2)).reshape(n_ex * tok, width)
    all_c = jnp.transpose(both[:, :, part:], (1, 0, 2)).reshape(n_ex * tok, width)

    gate_table = jnp.sum(
        jnp.where(
            routes[None, :, :] == lax.broadcasted_iota(jnp.int32, (n_ex, 1, 1), 0),
            route_gates[None, :, :],
            0.0,
        ),
        axis=2,
    )
    gate = lax.all_to_all(gate_table, "expert", split_axis=0, concat_axis=0, tiled=True)
    gate = gate.reshape(n_ex * tok, 1)
    copy_id = slab_owner[col] // slabs
    owner_block = lax.broadcasted_iota(jnp.int32, (n_ex, tok), 0).reshape(n_ex * tok, 1)
    both_weight = gate + (owner_block * copies // n_ex == copy_id).astype(F32)

    pre_gate = dot(all_x, w_gate, 1, 1)
    pre_up = dot(all_x, w_up, 1, 1)
    d_hidden = dot(all_c, w_down, 1, 1)
    act, slope = silu_parts(pre_gate)
    hidden = act * pre_up
    d_gate = d_hidden * pre_up * slope
    d_up = d_hidden * act

    out = dot((both_weight * hidden).astype(BF16), w_down, 1, 0).astype(BF16)
    back = (
        dot((both_weight * d_gate).astype(BF16), w_gate, 1, 0)
        + dot((both_weight * d_up).astype(BF16), w_up, 1, 0)
    ).astype(BF16)

    def grad(values, rows):
        ordered = jnp.dot((gate * values).astype(BF16), order, preferred_element_type=F32)
        return dot(ordered.astype(BF16), rows, 0, 0)

    weight_grads = jnp.stack(
        [grad(d_gate, all_x), grad(d_up, all_x), grad(hidden, all_c)]
    ).astype(BF16)[None]

    if out.size * out.dtype.itemsize <= 1 << 23:
        mixed, token_grad = halving_sum(n_dp, n_ex, [out, back])
    else:
        (mixed,) = halving_sum(n_dp, n_ex, [out])
        (token_grad,) = halving_sum(n_dp, n_ex, [back])
    return (mixed, token_grad, weight_grads)


def solution(mesh):
    in_specs = (
        P(None, "dp", "expert"),
        P("expert", None),
        P("expert", None),
        P("expert", None),
        P("expert", None),
        P(),
        P(),
    )
    out_specs = (P("expert", "dp"), P("expert", "dp"), P("expert", None, "dp", None))
    return jax.shard_map(body, mesh=mesh, in_specs=in_specs, out_specs=out_specs, check_vma=False)
```
